256 devices in a mesh: ctx: 32 (over z, y_hi, core), fsdp: 8 (over x, y_lo).
Axes of the slice: x: 4, y: 4 (y_hi: 2, y_lo: 2; y = y_hi * 2 + y_lo), z: 8, core: 2. Of those that a mesh axis runs over, the one named last changes fastest.
Arguments:
- xbc_raw: bfloat16 [8, 4096, 2560], P('fsdp', 'ctx'), may hold values from -6 to 6
- dt_raw: float32 [8, 4096, 64], P('fsdp', 'ctx'), as said below
- a_log: float32 [64], replicated, may hold values from 0 to 2.7726, as said below
- skip: float32 [64], replicated, may hold values from 0.5 to 1.5
- conv_weight: bfloat16 [4, 2560], P(None, 'fsdp'), may hold values from -3 to 3
- conv_bias: bfloat16 [2560], P('fsdp'), may hold values from -3 to 3
- grad_y: bfloat16 [8, 4096, 2048], P('fsdp', 'ctx'), may hold values from -6 to 6
Outputs:
- grad_xbc_raw: bfloat16 [8, 4096, 2560], P('fsdp', 'ctx')
- grad_dt_raw: float32 [8, 4096, 64], P('fsdp', 'ctx')
- grad_a_log: float32 [64], replicated
- grad_skip: float32 [64], replicated
- grad_conv_weight: float32 [4, 2560], P(None, 'fsdp')
- grad_conv_bias: float32 [2560], P('fsdp')
The draws below stay inside these ranges and needn't reach their ends.
Inputs may be any that keep to these rules, and one draw needn't show every extreme that they name: Each head's decay coefficient exp(a_log) lies between 1 and 16. softplus(dt_raw) is a positive step size.
All inputs are finite; a program needn't handle non-finite values.
Results may differ from the reference program's by a relative error of at most 0.0007.
Values may be sent and summed in bfloat16 or wider, within the bound.
A program may use at most 256 MiB of HBM per device.

```python
import math
import jax
import jax.numpy as jnp
from jax import lax

HW = 64
GW = 4
P_SIZE = 32
N = 64
KW = 4
SPAN = 128
CH = 2560
SEQUENCE_LENGTH = 4096
BATCH_COUNT = 8


def decay_tables(key):
    base_key = jax.random.fold_in(key, 101)
    random_key_list = jax.random.split(base_key, 8)
    fast_share = 0.5
    fast_heads = jax.random.bernoulli(random_key_list[0], fast_share, (HW,))
    a_log = jax.random.uniform(random_key_list[1], (HW,), jnp.float32, 0.0, math.log(16.0))
    fast_rate = 1.0 / 40.0 * jnp.exp(jax.random.uniform(random_key_list[2], (HW,), jnp.float32, math.log(0.75), math.log(1.33)))
    slow_rate = 0.7 / SEQUENCE_LENGTH * jnp.exp(jax.random.uniform(random_key_list[3], (HW,), jnp.float32, math.log(0.5), math.log(1.5)))
    head_frequency = jnp.where(fast_heads, fast_rate, slow_rate)
    positions = jnp.arange(SEQUENCE_LENGTH).astype(jnp.float32)
    phase_shift = jax.random.uniform(random_key_list[4], (BATCH_COUNT, 1), jnp.float32, -math.pi, math.pi)
    sinusoid_multiplier = jnp.exp(0.8 * jnp.sin(2.0 * math.pi * 3.0 * positions[None, :] / SEQUENCE_LENGTH + phase_shift))
    noise_multiplier = jax.random.uniform(random_key_list[5], (BATCH_COUNT, SEQUENCE_LENGTH, HW), jnp.float32, 0.5, 1.5)
    spike_positions = jax.random.randint(random_key_list[6], (BATCH_COUNT, 2), 0, SEQUENCE_LENGTH)
    spike_events = jnp.sum((jnp.arange(SEQUENCE_LENGTH)[None, :, None] == spike_positions[:, None, :]).astype(jnp.float32), -1)
    loss_fraction = jax.random.uniform(random_key_list[7], (BATCH_COUNT, 1, HW), jnp.float32, 0.2, 0.5)
    spike_probability = -jnp.log(1.0 - loss_fraction) * spike_events[..., None]
    token_values = head_frequency * sinusoid_multiplier[..., None] * noise_multiplier + spike_probability
    step_size = token_values / jnp.exp(a_log)
    dt_values = jnp.log(jnp.expm1(step_size))
    return (a_log, dt_values)


def draw_a_log(key, part):
    return decay_tables(key)[0]


def draw_dt_raw(key, part):
    return decay_tables(key)[1]


def block_scale(rng, dims, pieces, least, high):
    factor_of, own = 1.0, jax.random.fold_in(rng, 6)
    for axis_at, blocks in pieces:
        draws = jnp.exp(jax.random.uniform(jax.random.fold_in(own, axis_at), (blocks,), jnp.float32, least / len(pieces), high / len(pieces)))
        factor_of = factor_of * jnp.repeat(draws, dims[axis_at] // blocks).reshape([-1 if axis == axis_at else 1 for axis in range(len(dims))])
    return factor_of


def scatter_about(rng, shape, width, reach, cuts=(), held_as=jnp.bfloat16):
    factor_of = block_scale(rng, shape, cuts, -0.22, 0.18) if cuts else 1.0
    result = jax.random.normal(rng, shape, jnp.float32) * width * factor_of
    return jnp.minimum(jnp.maximum(result, -reach), reach).astype(held_as)


def setup_inputs(seed: int = 0) -> dict:
    key_list = jax.random.split(jax.random.key(seed), 8)
    xbc_raw = scatter_about(key_list[0], (BATCH_COUNT, SEQUENCE_LENGTH, CH), 1.0, 6.0, ((0, 8), (1, 32)))
    dt_raw = draw_dt_raw(jax.random.fold_in(key_list[7], 71), 0)
    a_log = draw_a_log(jax.random.fold_in(key_list[7], 71), 0)
    skip = jnp.clip(jax.random.uniform(key_list[3], (HW,), jnp.float32, 0.5, 1.5), 0.5, 1.5)
    conv_weight = scatter_about(key_list[4], (KW, CH), KW ** -0.5, 3.0, ((1, 8),))
    conv_bias = scatter_about(key_list[5], (CH,), 0.5, 3.0, ((0, 8),))
    grad_y = scatter_about(key_list[6], (BATCH_COUNT, SEQUENCE_LENGTH, HW * P_SIZE), 1.0, 6.0, ((0, 8), (1, 32)))
    return {"xbc_raw": xbc_raw, "dt_raw": dt_raw, "a_log": a_log, "skip": skip, "conv_weight": conv_weight, "conv_bias": conv_bias, "grad_y": grad_y}


HIGHEST_PREC = lax.Precision.HIGHEST

def sequence_forward(raw_rows, steps_raw, a_log, skip, weight_f, bias_f):
    length = raw_rows.shape[0]
    padded = jnp.concatenate([jnp.zeros((KW - 1, raw_rows.shape[1]), jnp.float32), raw_rows], 0)
    pre_act = bias_f + sum((weight_f[tap_idx] * padded[tap_idx:tap_idx + length] for tap_idx in range(KW)))
    conv_out = jax.nn.silu(pre_act)
    per_group = HW // GW
    inner_width = HW * P_SIZE
    blocks = length // SPAN
    x_all = conv_out[:, :inner_width].reshape(blocks, SPAN, GW, per_group, P_SIZE)
    b_all = conv_out[:, inner_width:inner_width + GW * N].reshape(blocks, SPAN, GW, N)
    c_all = conv_out[:, inner_width + GW * N:].reshape(blocks, SPAN, GW, N)
    step_size = jax.nn.softplus(steps_raw)
    log_decay = -jnp.exp(a_log) * step_size
    dt_all = step_size.reshape(blocks, SPAN, GW, per_group)
    la_all = log_decay.reshape(blocks, SPAN, GW, per_group)
    skip_heads = skip.reshape(GW, per_group)
    lower_mask = jnp.tril(jnp.ones((SPAN, SPAN), bool))

    def span_step(carried, seq_items):
        x_c, b_c, c_c, dt_c, la_c = seq_items
        cum_log = jnp.cumsum(la_c, 0)
        cum_t = jnp.transpose(cum_log, (1, 2, 0))
        log_gap = cum_t[..., :, None] - cum_t[..., None, :]
        mixing = jnp.where(lower_mask, jnp.exp(jnp.where(lower_mask, log_gap, 0.0)), 0.0)
        scores = jnp.einsum('tgn,sgn->gts', c_c, b_c, precision=HIGHEST_PREC)
        inputs = dt_c[..., None] * x_c
        span_out = jnp.einsum('gkts,sgkp->tgkp', scores[:, None] * mixing, inputs, precision=HIGHEST_PREC)
        span_out = span_out + jnp.exp(cum_log)[..., None] * jnp.einsum('tgn,gkpn->tgkp', c_c, carried, precision=HIGHEST_PREC)
        span_out = span_out + skip_heads[..., None] * x_c
        last_log = cum_log[-1]
        tail_decay = jnp.exp(last_log[None] - cum_log)
        next_state = jnp.exp(last_log)[..., None, None] * carried + jnp.einsum('sgkp,sgn->gkpn', tail_decay[..., None] * inputs, b_c, precision=HIGHEST_PREC)
        return (next_state, span_out)
    zero_state = jnp.zeros((GW, per_group, P_SIZE, N), jnp.float32)
    _, outputs = lax.scan(jax.checkpoint(span_step), zero_state, (x_all, b_all, c_all, dt_all, la_all))
    return outputs.reshape(length, inner_width)

def reference(xbc_raw, dt_raw, a_log, skip, conv_weight, conv_bias, grad_y):
    weight_f = conv_weight.astype(jnp.float32)
    bias_f = conv_bias.astype(jnp.float32)

    def per_sequence(seq_items):
        raw_rows, steps_raw, cotangent = seq_items
        _, pullback = jax.vjp(sequence_forward, raw_rows.astype(jnp.float32), steps_raw, a_log, skip, weight_f, bias_f)
        return pullback(cotangent.astype(jnp.float32))
    gradients = lax.map(per_sequence, (xbc_raw, dt_raw, grad_y))
    grad_scale = 1.0 / math.sqrt(BATCH_COUNT * SEQUENCE_LENGTH)
    return (gradients[0].astype(jnp.bfloat16), gradients[1], lax.optimization_barrier(jnp.sum(gradients[2], 0)) * grad_scale, lax.optimization_barrier(jnp.sum(gradients[3], 0)) * grad_scale, lax.optimization_barrier(jnp.sum(gradients[4], 0)) * grad_scale, lax.optimization_barrier(jnp.sum(gradients[5], 0)) * grad_scale)
```

```python
import math

import jax
import jax.numpy as jnp
from jax import lax
from jax.sharding import PartitionSpec as P

HW = 64
GW = 4
P_SIZE = 32
N = 64
KW = 4
SPAN = 128


HIGHEST_PREC = lax.Precision.HIGHEST


def from_behind(value, axis, by):
    length = lax.axis_size(axis)
    pairs = [(i, i + by) for i in range(length) if 0 <= i + by < length]
    return lax.ppermute(value, axis, pairs)


def compose(earlier, later):
    return (earlier[0] * later[0], later[0][..., None, None] * earlier[1] + later[1])


def exclusive_scans(fwd, bwd, axis):
    count = lax.axis_size(axis)
    width = 1
    while 2 * width < count:
        fwd = compose(from_behind(fwd, axis, width), fwd)
        bwd = compose(from_behind(bwd, axis, -width), bwd)
        width *= 2
    fwd_near = from_behind(fwd, axis, 1)
    bwd_near = from_behind(bwd, axis, -1)
    if width + 1 < count:
        fwd = compose(from_behind(fwd, axis, width + 1), fwd_near)
        bwd = compose(from_behind(bwd, axis, -(width + 1)), bwd_near)
    else:
        fwd, bwd = fwd_near, bwd_near
    return fwd[1], bwd[1]


def body(xbc_raw, dt_raw, a_log, skip, conv_weight, conv_bias, grad_y):
    raw_rows = xbc_raw[0]
    tok_rows = raw_rows.shape[0]
    per_group = HW // GW
    inner_width = HW * P_SIZE
    blocks = tok_rows // SPAN
    params_all = lax.all_gather(
        jnp.concatenate([conv_weight, conv_bias[None]], 0), "fsdp", axis=1, tiled=True
    ).astype(jnp.float32)
    weight_f = params_all[:KW]
    bias_f = params_all[KW]
    tail_rows = raw_rows[tok_rows - (KW - 1) :]
    rows_prev = from_behind(tail_rows, "ctx", 1)
    padded = jnp.concatenate([rows_prev, raw_rows], 0).astype(jnp.float32)
    pre_act = bias_f + sum(
        (weight_f[tap_idx] * padded[tap_idx : tap_idx + tok_rows] for tap_idx in range(KW))
    )
    gate_vals = jax.nn.sigmoid(pre_act)
    conv_out = pre_act * gate_vals
    x_all = conv_out[:, :inner_width].reshape(blocks, SPAN, GW, per_group, P_SIZE)
    b_all = conv_out[:, inner_width : inner_width + GW * N].reshape(blocks, SPAN, GW, N)
    c_all = conv_out[:, inner_width + GW * N :].reshape(blocks, SPAN, GW, N)
    steps_raw = dt_raw[0]
    step_size = jax.nn.softplus(steps_raw)
    rate_head = jnp.exp(a_log)
    log_decay = -rate_head * step_size
    dt_c = step_size.reshape(blocks, SPAN, GW, per_group)
    la_c = log_decay.reshape(blocks, SPAN, GW, per_group)
    d_out = grad_y[0].astype(jnp.float32).reshape(blocks, SPAN, GW, per_group, P_SIZE)
    cum_log = jnp.cumsum(la_c, 1)
    exp_cum = jnp.exp(cum_log)
    last_log = cum_log[:, -1]
    span_decay = jnp.exp(last_log)
    tail_decay = jnp.exp(last_log[:, None] - cum_log)
    inputs = dt_c[..., None] * x_all
    local_end = jnp.einsum(
        "csgkp,csgn->cgkpn", tail_decay[..., None] * inputs, b_all, precision=HIGHEST_PREC
    )
    local_adj = jnp.einsum(
        "ctgkp,ctgn->cgkpn", exp_cum[..., None] * d_out, c_all, precision=HIGHEST_PREC
    )
    unit_decay = jnp.ones((GW, per_group), jnp.float32)
    zero_state = jnp.zeros((GW, per_group, P_SIZE, N), jnp.float32)
    dev_decay = unit_decay
    fwd_total = zero_state
    span_idx = 0
    fwd_total = span_decay[span_idx][..., None, None] * fwd_total + local_end[span_idx]
    dev_decay = dev_decay * span_decay[span_idx]
    back_total = zero_state
    for span_idx in reversed(range(blocks)):
        back_total = local_adj[span_idx] + span_decay[span_idx][..., None, None] * back_total
    state_in, adjoint_end = exclusive_scans((dev_decay, fwd_total), (dev_decay, back_total), "ctx")
    cum_t = jnp.transpose(cum_log, (0, 2, 3, 1))
    lower_mask = jnp.tril(jnp.ones((SPAN, SPAN), bool))
    log_gap = cum_t[..., :, None] - cum_t[..., None, :]
    mixing = jnp.where(lower_mask, jnp.exp(jnp.where(lower_mask, log_gap, 0.0)), 0.0)
    scores = jnp.einsum("ctgn,csgn->cgts", c_all, b_all, precision=HIGHEST_PREC)
    weights = scores[:, :, None] * mixing
    d_weights = jnp.einsum("ctgkp,csgkp->cgkts", d_out, inputs, precision=HIGHEST_PREC)
    d_inputs = jnp.einsum("cgkts,ctgkp->csgkp", weights, d_out, precision=HIGHEST_PREC)
    flow_terms = d_weights * weights
    d_scores = jnp.sum(d_weights * mixing, 2)
    d_cum = jnp.transpose(jnp.sum(flow_terms, -1) - jnp.sum(flow_terms, -2), (0, 3, 1, 2))
    d_c = jnp.einsum("cgts,csgn->ctgn", d_scores, b_all, precision=HIGHEST_PREC)
    d_b = jnp.einsum("cgts,ctgn->csgn", d_scores, c_all, precision=HIGHEST_PREC)
    carried = state_in
    span_idx = 0
    start_list = [carried]
    end_list = []
    carried = adjoint_end
    for span_idx in reversed(range(blocks)):
        end_list.append(carried)
        carried = local_adj[span_idx] + span_decay[span_idx][..., None, None] * carried
    start_state = jnp.stack(start_list)
    end_adjoint = jnp.stack(end_list[::-1])
    from_state = jnp.einsum("ctgn,cgkpn->ctgkp", c_all, start_state, precision=HIGHEST_PREC)
    d_cum = d_cum + exp_cum * jnp.sum(d_out * from_state, -1)
    d_c = d_c + jnp.einsum(
        "ctgkp,cgkpn->ctgn", exp_cum[..., None] * d_out, start_state, precision=HIGHEST_PREC
    )
    pulled = jnp.einsum("cgkpn,csgn->csgkp", end_adjoint, b_all, precision=HIGHEST_PREC)
    d_inputs = d_inputs + tail_decay[..., None] * pulled
    d_b = d_b + jnp.einsum(
        "csgkp,cgkpn->csgn", tail_decay[..., None] * inputs, end_adjoint, precision=HIGHEST_PREC
    )
    d_tail = tail_decay * jnp.sum(inputs * pulled, -1)
    d_last = jnp.sum(d_tail, 1) + span_decay * jnp.sum(end_adjoint * start_state, (-2, -1))
    d_cum = d_cum - d_tail
    d_cum = d_cum.at[:, -1].add(d_last)
    d_log = jnp.flip(jnp.cumsum(jnp.flip(d_cum, 1), 1), 1)
    d_step = jnp.sum(d_inputs * x_all, -1) - rate_head.reshape(GW, per_group) * d_log
    d_x = d_inputs * dt_c[..., None] + skip.reshape(GW, per_group)[..., None] * d_out
    d_skip_local = jnp.sum(d_out * x_all, (0, 1, 4)).reshape(HW)
    d_alog_local = jnp.sum(d_log * la_c, (0, 1)).reshape(HW)
    d_dt_raw = d_step.reshape(tok_rows, HW) * jax.nn.sigmoid(steps_raw)
    d_conv = jnp.concatenate(
        [
            d_x.reshape(tok_rows, inner_width),
            d_b.reshape(tok_rows, GW * N),
            d_c.reshape(tok_rows, GW * N),
        ],
        1,
    )
    d_pre = d_conv * gate_vals * (1.0 + pre_act * (1.0 - gate_vals))
    rows_next = from_behind(d_pre[: KW - 1], "ctx", -1)
    extended = jnp.concatenate([d_pre, rows_next], 0)
    d_raw = sum(
        (
            weight_f[tap_idx] * extended[KW - 1 - tap_idx : KW - 1 - tap_idx + tok_rows]
            for tap_idx in range(KW)
        )
    )
    d_weight = jnp.stack(
        [jnp.sum(d_pre * padded[tap_idx : tap_idx + tok_rows], 0) for tap_idx in range(KW)]
    )
    d_bias = jnp.sum(d_pre, 0)
    grad_scale = 1.0 / math.sqrt(tok_rows * lax.axis_size("ctx") * lax.axis_size("fsdp"))
    channels = d_bias.shape[0]
    packed = jnp.concatenate(
        [d_weight.reshape(-1), d_bias, d_alog_local, d_skip_local]
    )
    packed = lax.psum(packed, ("ctx", "fsdp"))
    own = channels // lax.axis_size("fsdp")
    col0 = lax.axis_index("fsdp") * own
    wb = packed[: (KW + 1) * channels].reshape(KW + 1, channels)
    wb_own = lax.dynamic_slice_in_dim(wb, col0, own, axis=1)
    total_weight, total_bias = wb_own[:KW], wb_own[KW]
    heads_part = packed[(KW + 1) * channels :]
    head_alog, head_skip = heads_part[:HW], heads_part[HW:]
    return (
        d_raw.astype(jnp.bfloat16)[None],
        d_dt_raw[None],
        head_alog * grad_scale,
        head_skip * grad_scale,
        total_weight * grad_scale,
        total_bias * grad_scale,
    )


def solution(mesh):
    in_specs = (
        P("fsdp", "ctx", None),
        P("fsdp", "ctx", None),
        P(),
        P(),
        P(None, "fsdp"),
        P("fsdp"),
        P("fsdp", "ctx", None),
    )
    out_specs = (
        P("fsdp", "ctx", None),
        P("fsdp", "ctx", None),
        P(),
        P(),
        P(None, "fsdp"),
        P("fsdp"),
    )
    return jax.shard_map(body, mesh=mesh, in_specs=in_specs, out_specs=out_specs, check_vma=False)
```
